256 devices in a mesh: train: 16 (over z, core), query: 16 (over y, x).
Axes of the slice: x: 4, y: 4, z: 8, core: 2. Of those that a mesh axis runs over, the one named last changes fastest.
Arguments:
- train_hidden: bfloat16 [512, 96, 4096], P(('train', 'query')), may hold values from -6 to 6
- train_outgrad: bfloat16 [512, 96, 14336], P(('train', 'query')), may hold values from -6 to 6
- train_mask: int32 [512, 96], P(('train', 'query')), may hold values 0 or 1
- query_hidden: bfloat16 [256, 96, 4096], P(('train', 'query')), may hold values from -6 to 6
- query_outgrad: bfloat16 [256, 96, 14336], P(('train', 'query')), may hold values from -6 to 6
- query_mask: int32 [256, 96], P(('train', 'query')), may hold values 0 or 1
- proj_in: bfloat16 [4096, 64], replicated, may hold values from -0.09375 to 0.09375
- proj_out: bfloat16 [14336, 64], replicated, may hold values from -0.046875 to 0.046875
Outputs:
- scores: float32 [512, 256], P(('train', 'query'))
The draws below stay inside these ranges and needn't reach their ends.
All inputs are finite; a program needn't handle non-finite values. No bound on the sum of `train_mask` or of `query_mask` on one device may be relied on, other than what follows from the above.
Results may differ from the reference program's by a relative error of at most 0.0003.
Values sent between devices are 32-bit elements; how exact they have to be, the bound alone decides.
A program may use at most 128 MiB of HBM per device.

```python
import jax
import jax.numpy as jnp
from jax import lax

D = 4096
FF = 14336
RIN = 64
ROUT = 64
PROOF_LEN = 96
TRAINS = 512
QUERIES = 256


def set_ends(values, own_key, least, largest):
    dims = values.shape
    place = [jax.random.randint(jax.random.fold_in(own_key, axis), (), 0, dims[axis]) for axis in range(len(dims))]
    values = values.at[tuple(place)].set(least)
    longest = dims.index(max(dims))
    place[longest] = (place[longest] + 1) % dims[longest]
    return values.at[tuple(place)].set(largest)


def shard_levels(own_key, extent, split, smallest, top_value):
    gain = 1.0
    for position, blocks in split:
        steps = jax.random.uniform(jax.random.fold_in(jax.random.fold_in(own_key, 6), position), (blocks,), jnp.float32, smallest / len(split), top_value / len(split))
        gain = gain * jnp.repeat(jnp.exp(steps), extent[position] // blocks).reshape((-1,) + (1,) * (len(extent) - 1 - position))
    return gain


def noise(key, extent, scale, limit, split=(), held_as=jnp.bfloat16):
    result = jax.random.normal(key, extent, jnp.float32) * scale
    if len(split) > 0:
        result = shard_levels(key, extent, split, -0.22, 0.18) * result
    return jnp.clip(result, min=-limit, max=limit).astype(held_as)


def setup_inputs(seed: int = 0) -> dict:
    streams_of = jax.random.split(jax.random.key(seed), 9)
    train_hidden = noise(streams_of[0], (TRAINS, PROOF_LEN, D), 1.0, 6.0, ((0, 256),))
    train_outgrad = noise(streams_of[1], (TRAINS, PROOF_LEN, FF), 1.0, 6.0, ((0, 256),))
    train_mask = set_ends((jax.random.randint(streams_of[2], (TRAINS, PROOF_LEN), 0, 4) < 3).astype(jnp.int32), jax.random.fold_in(streams_of[2], 1), 0, 1)
    query_hidden = noise(streams_of[3], (QUERIES, PROOF_LEN, D), 1.0, 6.0, ((0, 256),))
    query_outgrad = noise(streams_of[4], (QUERIES, PROOF_LEN, FF), 1.0, 6.0, ((0, 256),))
    query_mask = set_ends((jax.random.randint(streams_of[5], (QUERIES, PROOF_LEN), 0, 2) < 1).astype(jnp.int32), jax.random.fold_in(streams_of[5], 1), 0, 1)
    proj_in = noise(streams_of[6], (D, RIN), D ** -0.5, 0.09375)
    proj_out = noise(streams_of[7], (FF, ROUT), FF ** -0.5, 0.046875)
    return dict(train_hidden=train_hidden, train_outgrad=train_outgrad, train_mask=train_mask, query_hidden=query_hidden, query_outgrad=query_outgrad, query_mask=query_mask, proj_in=proj_in, proj_out=proj_out)


damping_share = 0.1

def project(hidden, outgrad, mask, proj_in, proj_out):

    def one_proof(pieces):
        hidden_rows, outgrad_rows, mask_row = pieces
        input_side = jnp.dot(hidden_rows.astype(jnp.float32), proj_in.astype(jnp.float32), preferred_element_type=jnp.float32)
        output_side = jnp.dot(outgrad_rows.astype(jnp.float32), proj_out.astype(jnp.float32), preferred_element_type=jnp.float32)
        output_side = output_side * mask_row.astype(jnp.float32)[:, None]
        return jnp.dot(output_side.T, input_side, precision=lax.Precision.HIGHEST).reshape(-1)
    return lax.map(one_proof, (hidden, outgrad, mask))

def chol_solve(factor, right):
    lower_solved = lax.linalg.triangular_solve(factor, right, left_side=True, lower=True)
    return lax.linalg.triangular_solve(factor, lower_solved, left_side=True, lower=True, transpose_a=True)

def reference(train_hidden, train_outgrad, train_mask, query_hidden, query_outgrad, query_mask, proj_in, proj_out):
    train_sketch = project(train_hidden, train_outgrad, train_mask, proj_in, proj_out)
    query_sketch = project(query_hidden, query_outgrad, query_mask, proj_in, proj_out)
    gram_matrix = jnp.dot(train_sketch, train_sketch.T, precision=lax.Precision.HIGHEST)
    products = jnp.dot(train_sketch, query_sketch.T, precision=lax.Precision.HIGHEST)
    total_rows = train_sketch.shape[0]
    damping = damping_share * jnp.trace(gram_matrix) / total_rows
    system = gram_matrix + damping * jnp.eye(total_rows, dtype=jnp.float32)
    factor = jnp.linalg.cholesky(system)
    return total_rows * chol_solve(factor, products)
```

```python
import jax
import jax.numpy as jnp
from jax import lax
from jax.sharding import PartitionSpec as P

damping_share = 0.1
AXES = ("train", "query")


def sketch_terms(hidden, outgrad, mask, proj_in, proj_out):
    proof_count, token_count, model_width = hidden.shape
    input_side = jnp.dot(
        hidden.reshape(proof_count * token_count, model_width),
        proj_in,
        preferred_element_type=jnp.float32,
    )
    output_side = jnp.dot(
        outgrad.reshape(proof_count * token_count, -1), proj_out, preferred_element_type=jnp.float32
    )
    output_side = output_side * mask.reshape(-1, 1).astype(jnp.float32)
    input_side = input_side.reshape(proof_count, token_count, -1)
    output_side = output_side.reshape(proof_count, token_count, -1)
    outer_sum = jnp.einsum("pti,ptj->pij", output_side, input_side, precision=lax.Precision.HIGHEST)
    return outer_sum.reshape(proof_count, -1)


def chol_solve(factor, right):
    lower_solved = lax.linalg.triangular_solve(factor, right, left_side=True, lower=True)
    return lax.linalg.triangular_solve(
        factor, lower_solved, left_side=True, lower=True, transpose_a=True
    )


def body(
    train_hidden,
    train_outgrad,
    train_mask,
    query_hidden,
    query_outgrad,
    query_mask,
    proj_in,
    proj_out,
):
    train_sketch = sketch_terms(train_hidden, train_outgrad, train_mask, proj_in, proj_out)
    query_sketch = sketch_terms(query_hidden, query_outgrad, query_mask, proj_in, proj_out)
    block_rows = train_sketch.shape[0]
    query_rows = query_sketch.shape[0]
    devices = lax.axis_size(AXES)
    width = train_sketch.shape[1]
    chunk = width // devices
    rows = jnp.concatenate([train_sketch, query_sketch], axis=0)
    pieces = rows.reshape(block_rows + query_rows, devices, chunk).transpose(1, 0, 2)
    gathered = lax.all_to_all(pieces, AXES, 0, 0, tiled=True)
    train_cols = gathered[:, :block_rows, :].reshape(devices * block_rows, chunk)
    query_cols = gathered[:, block_rows:, :].reshape(devices * query_rows, chunk)
    both_cols = jnp.concatenate([train_cols, query_cols], axis=0)
    partial = jnp.dot(train_cols, both_cols.T, precision=lax.Precision.HIGHEST)
    summed = lax.psum(partial, AXES)
    total_rows = devices * block_rows
    gram_matrix = summed[:, :total_rows]
    products = summed[:, total_rows:]
    damping = damping_share * jnp.trace(gram_matrix) / total_rows
    system = gram_matrix + damping * jnp.eye(total_rows, dtype=jnp.float32)
    factor = jnp.linalg.cholesky(system)
    solved = total_rows * chol_solve(factor, products)
    return lax.dynamic_slice_in_dim(
        solved, lax.axis_index(AXES) * block_rows, block_rows, 0
    )


def solution(mesh):
    in_specs = (
        P(AXES, None, None),
        P(AXES, None, None),
        P(AXES, None),
        P(AXES, None, None),
        P(AXES, None, None),
        P(AXES, None),
        P(),
        P(),
    )
    out_specs = P(AXES, None)
    return jax.shard_map(body, mesh=mesh, in_specs=in_specs, out_specs=out_specs, check_vma=False)
```

```python
import jax
import jax.numpy as jnp
from jax import lax
from jax.sharding import PartitionSpec as P

damping_share = 0.1
AXES = ("train", "query")


def sketch_terms(hidden, outgrad, mask, proj_in, proj_out):
    proof_count, token_count, model_width = hidden.shape
    input_side = jnp.dot(
        hidden.reshape(proof_count * token_count, model_width),
        proj_in,
        preferred_element_type=jnp.float32,
    )
    output_side = jnp.dot(
        outgrad.reshape(proof_count * token_count, -1), proj_out, preferred_element_type=jnp.float32
    )
    output_side = output_side * mask.reshape(-1, 1).astype(jnp.float32)
    input_side = input_side.reshape(proof_count, token_count, -1)
    output_side = output_side.reshape(proof_count, token_count, -1)
    outer_sum = jnp.einsum("pti,ptj->pij", output_side, input_side, precision=lax.Precision.HIGHEST)
    return outer_sum.reshape(proof_count, -1)


def chol_solve(factor, right):
    lower_solved = lax.linalg.triangular_solve(factor, right, left_side=True, lower=True)
    return lax.linalg.triangular_solve(
        factor, lower_solved, left_side=True, lower=True, transpose_a=True
    )


def body(
    train_hidden,
    train_outgrad,
    train_mask,
    query_hidden,
    query_outgrad,
    query_mask,
    proj_in,
    proj_out,
):
    train_sketch = sketch_terms(train_hidden, train_outgrad, train_mask, proj_in, proj_out)
    query_sketch = sketch_terms(query_hidden, query_outgrad, query_mask, proj_in, proj_out)
    block_rows = train_sketch.shape[0]
    query_block = query_sketch.shape[0]
    outer = lax.axis_size("train")
    inner = lax.axis_size("query")
    group_rows = lax.all_gather(train_sketch, "query", axis=0, tiled=True)
    both = jnp.concatenate([train_sketch, query_sketch], axis=0)
    column_rows = lax.all_gather(both, "train", axis=0, tiled=False)
    column_rows = column_rows.reshape(outer * (block_rows + query_block), -1)
    block = jnp.dot(group_rows, column_rows.T, precision=lax.Precision.HIGHEST)
    blocks = lax.all_gather(block, AXES, axis=0, tiled=False)
    group = inner * block_rows
    blocks = blocks.reshape(outer, inner, group, outer, block_rows + query_block)
    gram_matrix = (
        blocks[..., :block_rows]
        .transpose(0, 2, 3, 1, 4)
        .reshape(outer * group, outer * inner * block_rows)
    )
    products = (
        blocks[..., block_rows:]
        .transpose(0, 2, 3, 1, 4)
        .reshape(outer * group, outer * inner * query_block)
    )
    total_rows = gram_matrix.shape[0]
    damping = damping_share * jnp.trace(gram_matrix) / total_rows
    system = gram_matrix + damping * jnp.eye(total_rows, dtype=jnp.float32)
    factor = jnp.linalg.cholesky(system)
    solved = total_rows * chol_solve(factor, products)
    return lax.dynamic_slice_in_dim(
        solved, lax.axis_index(AXES) * block_rows, block_rows, 0
    )


def solution(mesh):
    in_specs = (
        P(AXES, None, None),
        P(AXES, None, None),
        P(AXES, None),
        P(AXES, None, None),
        P(AXES, None, None),
        P(AXES, None),
        P(),
        P(),
    )
    out_specs = P(AXES, None)
    return jax.shard_map(body, mesh=mesh, in_specs=in_specs, out_specs=out_specs, check_vma=False)
```

```python
import jax
import jax.numpy as jnp
from jax import lax
from jax.sharding import PartitionSpec as P

damping_share = 0.1
AXES = ("train", "query")
HIGHEST = lax.Precision.HIGHEST


def sketch_terms(hidden, outgrad, mask, proj_in, proj_out):
    proof_count, token_count, model_width = hidden.shape
    input_side = jnp.dot(
        hidden.reshape(proof_count * token_count, model_width),
        proj_in,
        preferred_element_type=jnp.float32,
    )
    output_side = jnp.dot(
        outgrad.reshape(proof_count * token_count, -1), proj_out, preferred_element_type=jnp.float32
    )
    output_side = output_side * mask.reshape(-1, 1).astype(jnp.float32)
    input_side = input_side.reshape(proof_count, token_count, -1)
    output_side = output_side.reshape(proof_count, token_count, -1)
    outer_sum = jnp.einsum("pti,ptj->pij", output_side, input_side, precision=HIGHEST)
    return outer_sum.reshape(proof_count, -1)


def spd_solve(system, right, tolerance=1e-3, most_steps=48):
    size = system.shape[0]
    diagonal = jnp.diagonal(system)
    inv_sqrt = lax.rsqrt(diagonal)
    bound = jnp.max(jnp.sum(jnp.abs(system) * inv_sqrt[:, None] * inv_sqrt[None, :], axis=1))
    eye = jnp.eye(size, dtype=system.dtype)
    start = eye * (1.0 / (diagonal * bound))[None, :]

    def going(carry):
        step, _, residual = carry
        return (step < most_steps) & (residual > tolerance)

    def advance(carry):
        step, inverse, _ = carry
        remainder = eye - jnp.dot(system, inverse, precision=HIGHEST)
        residual = jnp.max(jnp.abs(remainder))
        return step + 1, inverse + jnp.dot(inverse, remainder, precision=HIGHEST), residual

    _, inverse, _ = lax.while_loop(
        going, advance, (jnp.int32(0), start, jnp.array(jnp.inf, system.dtype))
    )
    solved = jnp.dot(inverse, right, precision=HIGHEST)
    return solved + jnp.dot(
        inverse, right - jnp.dot(system, solved, precision=HIGHEST), precision=HIGHEST
    )


def body(
    train_hidden,
    train_outgrad,
    train_mask,
    query_hidden,
    query_outgrad,
    query_mask,
    proj_in,
    proj_out,
):
    train_sketch = sketch_terms(train_hidden, train_outgrad, train_mask, proj_in, proj_out)
    query_sketch = sketch_terms(query_hidden, query_outgrad, query_mask, proj_in, proj_out)
    block_rows = train_sketch.shape[0]
    width = train_sketch.shape[1]
    both = jnp.concatenate([train_sketch, query_sketch], axis=0)
    everyone = lax.all_gather(both, AXES, axis=0, tiled=False)
    all_train = everyone[:, :block_rows].reshape(-1, width)
    all_queries = everyone[:, block_rows:].reshape(-1, width)
    gram_matrix = jnp.dot(all_train, all_train.T, precision=HIGHEST)
    products = jnp.dot(all_train, all_queries.T, precision=HIGHEST)
    total_rows = gram_matrix.shape[0]
    damping = damping_share * jnp.trace(gram_matrix) / total_rows
    system = gram_matrix + damping * jnp.eye(total_rows, dtype=jnp.float32)
    solved = total_rows * spd_solve(system, products)
    return lax.dynamic_slice_in_dim(
        solved, lax.axis_index(AXES) * block_rows, block_rows, 0
    )


def solution(mesh):
    in_specs = (
        P(AXES, None, None),
        P(AXES, None, None),
        P(AXES, None),
        P(AXES, None, None),
        P(AXES, None, None),
        P(AXES, None),
        P(),
        P(),
    )
    out_specs = P(AXES, None)
    return jax.shard_map(body, mesh=mesh, in_specs=in_specs, out_specs=out_specs, check_vma=False)
```

```python
import jax
import jax.numpy as jnp
from jax import lax
from jax.sharding import PartitionSpec as P

damping_share = 0.1
AXES = ("train", "query")
HIGHEST = lax.Precision.HIGHEST


def sketch_terms(hidden, outgrad, mask, proj_in, proj_out):
    proof_count, token_count, model_width = hidden.shape
    input_side = jnp.dot(
        hidden.reshape(proof_count * token_count, model_width),
        proj_in,
        preferred_element_type=jnp.float32,
    )
    output_side = jnp.dot(
        outgrad.reshape(proof_count * token_count, -1), proj_out, preferred_element_type=jnp.float32
    )
    output_side = output_side * mask.reshape(-1, 1).astype(jnp.float32)
    input_side = input_side.reshape(proof_count, token_count, -1)
    output_side = output_side.reshape(proof_count, token_count, -1)
    outer_sum = jnp.einsum("pti,ptj->pij", output_side, input_side, precision=HIGHEST)
    return outer_sum.reshape(proof_count, -1)


def spd_solve(system, right, coarse_until=1e-2, tolerance=1e-3, most_steps=48):
    size = system.shape[0]
    eye = jnp.eye(size, dtype=system.dtype)
    diagonal = jnp.sum(system * eye, axis=1)
    inv_sqrt = lax.rsqrt(diagonal)
    bound = jnp.max(jnp.sum(jnp.abs(system) * inv_sqrt[:, None] * inv_sqrt[None, :], axis=1))
    start = eye * (1.0 / (diagonal * bound))[None, :]

    def stepper(precision):
        def advance(carry):
            step, inverse, _ = carry
            remainder = eye - jnp.dot(system, inverse, precision=precision)
            residual = jnp.sqrt(jnp.sum(remainder * remainder))
            return step + 1, inverse + jnp.dot(inverse, remainder, precision=precision), residual
        return advance

    def until(level):
        def going(carry):
            step, _, residual = carry
            return (step < most_steps) & (residual > level)
        return going

    carry = (jnp.int32(0), start, jnp.array(jnp.inf, system.dtype))
    carry = lax.while_loop(until(coarse_until), stepper(lax.Precision.HIGH), carry)
    carry = (carry[0], carry[1], jnp.array(jnp.inf, system.dtype))
    _, inverse, _ = lax.while_loop(until(tolerance), stepper(HIGHEST), carry)
    solved = jnp.dot(inverse, right, precision=HIGHEST)
    return solved + jnp.dot(
        inverse, right - jnp.dot(system, solved, precision=HIGHEST), precision=HIGHEST
    )


def body(
    train_hidden,
    train_outgrad,
    train_mask,
    query_hidden,
    query_outgrad,
    query_mask,
    proj_in,
    proj_out,
):
    train_sketch = sketch_terms(train_hidden, train_outgrad, train_mask, proj_in, proj_out)
    query_sketch = sketch_terms(query_hidden, query_outgrad, query_mask, proj_in, proj_out)
    block_rows = train_sketch.shape[0]
    both = jnp.concatenate([train_sketch, query_sketch], axis=0)
    everyone = lax.all_gather(both[:, None, :], AXES, axis=1, tiled=True)
    devices = everyone.shape[1]
    all_train = everyone[:block_rows].reshape(block_rows * devices, -1)
    all_queries = everyone[block_rows:].reshape(-1, everyone.shape[2])
    gram_matrix = jnp.dot(all_train, all_train.T, precision=HIGHEST)
    products = jnp.dot(all_train, all_queries.T, precision=HIGHEST)
    total_rows = gram_matrix.shape[0]
    eye = jnp.eye(total_rows, dtype=jnp.float32)
    damping = damping_share * jnp.sum(gram_matrix * eye) / total_rows
    system = gram_matrix + damping * eye
    solved = total_rows * spd_solve(system, products)
    me = lax.axis_index(AXES)
    return jnp.concatenate(
        [lax.dynamic_slice_in_dim(solved, r * devices + me, 1, 0) for r in range(block_rows)],
        axis=0,
    )


def solution(mesh):
    in_specs = (
        P(AXES, None, None),
        P(AXES, None, None),
        P(AXES, None),
        P(AXES, None, None),
        P(AXES, None, None),
        P(AXES, None),
        P(),
        P(),
    )
    out_specs = P(AXES, None)
    return jax.shard_map(body, mesh=mesh, in_specs=in_specs, out_specs=out_specs, check_vma=False)
```

```python
import jax
import jax.numpy as jnp
from jax import lax
from jax.sharding import PartitionSpec as P

damping_share = 0.1
AXES = ("train", "query")
HIGHEST = lax.Precision.HIGHEST


def sketch_terms(hidden, outgrad, mask, proj_in, proj_out):
    proof_count, token_count, model_width = hidden.shape
    input_side = jnp.dot(
        hidden.reshape(proof_count * token_count, model_width),
        proj_in,
        preferred_element_type=jnp.float32,
    )
    output_side = jnp.dot(
        outgrad.reshape(proof_count * token_count, -1), proj_out, preferred_element_type=jnp.float32
    )
    output_side = output_side * mask.reshape(-1, 1).astype(jnp.float32)
    input_side = input_side.reshape(proof_count, token_count, -1)
    output_side = output_side.reshape(proof_count, token_count, -1)
    outer_sum = jnp.einsum("pti,ptj->pij", output_side, input_side, precision=HIGHEST)
    return outer_sum.reshape(proof_count, -1)


def spd_solve(system, right, tolerance=1e-3, most_steps=48):
    size = system.shape[0]
    eye = jnp.eye(size, dtype=system.dtype)
    diagonal = jnp.sum(system * eye, axis=1)
    inv_sqrt = lax.rsqrt(diagonal)
    bound = jnp.max(jnp.sum(jnp.abs(system) * inv_sqrt[:, None] * inv_sqrt[None, :], axis=1))
    start = eye * (1.0 / (diagonal * bound))[None, :]

    def going(carry):
        step, _, residual = carry
        return (step < most_steps) & (residual > tolerance)

    def advance(carry):
        step, inverse, _ = carry
        remainder = eye - jnp.dot(system, inverse, precision=HIGHEST)
        residual = jnp.sqrt(jnp.sum(remainder * remainder))
        return step + 1, inverse + jnp.dot(inverse, remainder, precision=HIGHEST), residual

    _, inverse, _ = lax.while_loop(
        going, advance, (jnp.int32(0), start, jnp.array(jnp.inf, system.dtype))
    )
    solved = jnp.dot(inverse, right, precision=HIGHEST)
    return solved + jnp.dot(
        inverse, right - jnp.dot(system, solved, precision=HIGHEST), precision=HIGHEST
    )


def body(
    train_hidden,
    train_outgrad,
    train_mask,
    query_hidden,
    query_outgrad,
    query_mask,
    proj_in,
    proj_out,
):
    train_sketch = sketch_terms(train_hidden, train_outgrad, train_mask, proj_in, proj_out)
    query_sketch = sketch_terms(query_hidden, query_outgrad, query_mask, proj_in, proj_out)
    block_rows = train_sketch.shape[0]
    width = train_sketch.shape[1]
    both = jnp.concatenate([train_sketch, query_sketch], axis=0)
    everyone = lax.all_gather(both.reshape(1, -1), AXES, axis=0, tiled=True)
    devices = everyone.shape[0]
    pieces = [everyone[:, r * width:(r + 1) * width] for r in range(block_rows + 1)]
    gram_matrix = jnp.concatenate(
        [
            jnp.concatenate(
                [jnp.dot(pieces[r], pieces[c].T, precision=HIGHEST) for c in range(block_rows)],
                axis=1,
            )
            for r in range(block_rows)
        ],
        axis=0,
    )
    products = jnp.concatenate(
        [jnp.dot(pieces[r], pieces[block_rows].T, precision=HIGHEST) for r in range(block_rows)],
        axis=0,
    )
    total_rows = gram_matrix.shape[0]
    eye = jnp.eye(total_rows, dtype=jnp.float32)
    damping = damping_share * jnp.sum(gram_matrix * eye) / total_rows
    system = gram_matrix + damping * eye
    solved = total_rows * spd_solve(system, products)
    me = lax.axis_index(AXES)
    return jnp.concatenate(
        [lax.dynamic_slice_in_dim(solved, r * devices + me, 1, 0) for r in range(block_rows)],
        axis=0,
    )


def solution(mesh):
    in_specs = (
        P(AXES, None, None),
        P(AXES, None, None),
        P(AXES, None),
        P(AXES, None, None),
        P(AXES, None, None),
        P(AXES, None),
        P(),
        P(),
    )
    out_specs = P(AXES, None)
    return jax.shard_map(body, mesh=mesh, in_specs=in_specs, out_specs=out_specs, check_vma=False)
```

```python
import jax
import jax.numpy as jnp
from jax import lax
from jax.sharding import PartitionSpec as P

damping_share = 0.1
AXES = ("train", "query")
HIGHEST = lax.Precision.HIGHEST


def sketch_terms(hidden, outgrad, mask, proj_in, proj_out):
    proof_count, token_count, model_width = hidden.shape
    input_side = jnp.dot(
        hidden.reshape(proof_count * token_count, model_width),
        proj_in,
        preferred_element_type=jnp.float32,
    )
    output_side = jnp.dot(
        outgrad.reshape(proof_count * token_count, -1), proj_out, preferred_element_type=jnp.float32
    )
    output_side = output_side * mask.reshape(-1, 1).astype(jnp.float32)
    input_side = input_side.reshape(proof_count, token_count, -1)
    output_side = output_side.reshape(proof_count, token_count, -1)
    outer_sum = jnp.einsum("pti,ptj->pij", output_side, input_side, precision=HIGHEST)
    return outer_sum.reshape(proof_count, -1)


def spd_solve(system, right, tolerance=1e-3, most_steps=48):
    size = system.shape[0]
    eye = jnp.eye(size, dtype=system.dtype)
    diagonal = jnp.sum(system * eye, axis=1)
    inv_sqrt = lax.rsqrt(diagonal)
    bound = jnp.max(jnp.sum(jnp.abs(system) * inv_sqrt[:, None] * inv_sqrt[None, :], axis=1))
    start = eye * (1.0 / (diagonal * bound))[None, :]

    def going(carry):
        step, _, residual = carry
        return (step < most_steps) & (residual > tolerance)

    def advance(carry):
        step, inverse, _ = carry
        remainder = eye - jnp.dot(system, inverse, precision=HIGHEST)
        residual = jnp.sqrt(jnp.sum(remainder * remainder))
        return step + 1, inverse + jnp.dot(inverse, remainder, precision=HIGHEST), residual

    _, inverse, _ = lax.while_loop(
        going, advance, (jnp.int32(0), start, jnp.array(jnp.inf, system.dtype))
    )
    solved = jnp.dot(inverse, right, precision=HIGHEST)
    return solved + jnp.dot(
        inverse, right - jnp.dot(system, solved, precision=HIGHEST), precision=HIGHEST
    )


def body(
    train_hidden,
    train_outgrad,
    train_mask,
    query_hidden,
    query_outgrad,
    query_mask,
    proj_in,
    proj_out,
):
    train_sketch = sketch_terms(train_hidden, train_outgrad, train_mask, proj_in, proj_out)
    query_sketch = sketch_terms(query_hidden, query_outgrad, query_mask, proj_in, proj_out)
    block_rows = train_sketch.shape[0]
    width = train_sketch.shape[1]
    both = jnp.concatenate([train_sketch, query_sketch], axis=0)
    within = lax.all_gather(both.reshape(1, -1), AXES[1], axis=0, tiled=True)
    everyone = lax.all_gather(within, AXES[0], axis=0, tiled=True)
    devices = everyone.shape[0]
    pieces = [everyone[:, r * width:(r + 1) * width] for r in range(block_rows + 1)]
    gram_matrix = jnp.concatenate(
        [
            jnp.concatenate(
                [jnp.dot(pieces[r], pieces[c].T, precision=HIGHEST) for c in range(block_rows)],
                axis=1,
            )
            for r in range(block_rows)
        ],
        axis=0,
    )
    products = jnp.concatenate(
        [jnp.dot(pieces[r], pieces[block_rows].T, precision=HIGHEST) for r in range(block_rows)],
        axis=0,
    )
    total_rows = gram_matrix.shape[0]
    eye = jnp.eye(total_rows, dtype=jnp.float32)
    damping = damping_share * jnp.sum(gram_matrix * eye) / total_rows
    system = gram_matrix + damping * eye
    solved = total_rows * spd_solve(system, products)
    me = lax.axis_index(AXES)
    return jnp.concatenate(
        [lax.dynamic_slice_in_dim(solved, r * devices + me, 1, 0) for r in range(block_rows)],
        axis=0,
    )


def solution(mesh):
    in_specs = (
        P(AXES, None, None),
        P(AXES, None, None),
        P(AXES, None),
        P(AXES, None, None),
        P(AXES, None, None),
        P(AXES, None),
        P(),
        P(),
    )
    out_specs = P(AXES, None)
    return jax.shard_map(body, mesh=mesh, in_specs=in_specs, out_specs=out_specs, check_vma=False)
```

```python
import jax
import jax.numpy as jnp
from jax import lax
from jax.sharding import PartitionSpec as P

damping_share = 0.1
AXES = ("train", "query")
HIGHEST = lax.Precision.HIGHEST


def sketch_terms(hidden, outgrad, mask, proj_in, proj_out):
    proof_count, token_count, model_width = hidden.shape
    input_side = jnp.dot(
        hidden.reshape(proof_count * token_count, model_width),
        proj_in,
        preferred_element_type=jnp.float32,
    )
    output_side = jnp.dot(
        outgrad.reshape(proof_count * token_count, -1), proj_out, preferred_element_type=jnp.float32
    )
    output_side = output_side * mask.reshape(-1, 1).astype(jnp.float32)
    input_side = input_side.reshape(proof_count, token_count, -1)
    output_side = output_side.reshape(proof_count, token_count, -1)
    outer_sum = jnp.einsum("pti,ptj->pij", output_side, input_side, precision=HIGHEST)
    return outer_sum.reshape(proof_count, -1)


def spd_solve(system, right, tolerance=1e-3, most_steps=48):
    size = system.shape[0]
    eye = jnp.eye(size, dtype=system.dtype)
    diagonal = jnp.sum(system * eye, axis=1)
    inv_sqrt = lax.rsqrt(diagonal)
    bound = jnp.max(jnp.sum(jnp.abs(system) * inv_sqrt[:, None] * inv_sqrt[None, :], axis=1))
    start = eye * (1.0 / (diagonal * bound))[None, :]

    def going(carry):
        step, _, residual = carry
        return (step < most_steps) & (residual > tolerance)

    def advance(carry):
        step, inverse, _ = carry
        remainder = eye - jnp.dot(system, inverse, precision=HIGHEST)
        residual = jnp.sqrt(jnp.sum(remainder * remainder))
        return step + 1, inverse + jnp.dot(inverse, remainder, precision=HIGHEST), residual

    _, inverse, _ = lax.while_loop(
        going, advance, (jnp.int32(0), start, jnp.array(jnp.inf, system.dtype))
    )
    solved = jnp.dot(inverse, right, precision=HIGHEST)
    return solved + jnp.dot(
        inverse, right - jnp.dot(system, solved, precision=HIGHEST), precision=HIGHEST
    )


def body(
    train_hidden,
    train_outgrad,
    train_mask,
    query_hidden,
    query_outgrad,
    query_mask,
    proj_in,
    proj_out,
):
    train_sketch = sketch_terms(train_hidden, train_outgrad, train_mask, proj_in, proj_out)
    query_sketch = sketch_terms(query_hidden, query_outgrad, query_mask, proj_in, proj_out)
    block_rows = train_sketch.shape[0]
    width = train_sketch.shape[1]
    both = jnp.concatenate([train_sketch, query_sketch], axis=0)
    within = lax.all_gather(both.reshape(1, -1), AXES[1], axis=0, tiled=True)
    everyone = lax.all_gather(within, AXES[0], axis=0, tiled=True)
    devices = everyone.shape[0]
    pieces = [everyone[:, r * width:(r + 1) * width] for r in range(block_rows + 1)]
    gram_matrix = jnp.concatenate(
        [
            jnp.concatenate(
                [jnp.dot(pieces[r], pieces[c].T, precision=HIGHEST) for c in range(block_rows)],
                axis=1,
            )
            for r in range(block_rows)
        ],
        axis=0,
    )
    products = jnp.concatenate(
        [jnp.dot(pieces[r], pieces[block_rows].T, precision=HIGHEST) for r in range(block_rows)],
        axis=0,
    )
    total_rows = gram_matrix.shape[0]
    eye = jnp.eye(total_rows, dtype=jnp.float32)
    damping = damping_share * jnp.sum(gram_matrix * eye) / total_rows
    system = gram_matrix + damping * eye
    system, products = lax.optimization_barrier((system, products))
    solved = total_rows * spd_solve(system, products)
    me = lax.axis_index(AXES)
    return jnp.concatenate(
        [lax.dynamic_slice_in_dim(solved, r * devices + me, 1, 0) for r in range(block_rows)],
        axis=0,
    )


def solution(mesh):
    in_specs = (
        P(AXES, None, None),
        P(AXES, None, None),
        P(AXES, None),
        P(AXES, None, None),
        P(AXES, None, None),
        P(AXES, None),
        P(),
        P(),
    )
    out_specs = P(AXES, None)
    return jax.shard_map(body, mesh=mesh, in_specs=in_specs, out_specs=out_specs, check_vma=False)
```

```python
import jax
import jax.numpy as jnp
from jax import lax
from jax.sharding import PartitionSpec as P

damping_share = 0.1
AXES = ("train", "query")
HIGHEST = lax.Precision.HIGHEST


def sketch_terms(hidden, outgrad, mask, proj_in, proj_out):
    proof_count, token_count, model_width = hidden.shape
    input_side = jnp.dot(
        hidden.reshape(proof_count * token_count, model_width),
        proj_in,
        preferred_element_type=jnp.float32,
    )
    output_side = jnp.dot(
        outgrad.reshape(proof_count * token_count, -1), proj_out, preferred_element_type=jnp.float32
    )
    output_side = output_side * mask.reshape(-1, 1).astype(jnp.float32)
    input_side = input_side.reshape(proof_count, token_count, -1)
    output_side = output_side.reshape(proof_count, token_count, -1)
    outer_sum = jnp.einsum("pti,ptj->pij", output_side, input_side, precision=HIGHEST)
    return outer_sum.reshape(proof_count, -1)


def spd_solve(system, right, tolerance=1e-3, most_steps=48):
    size = system.shape[0]
    eye = jnp.eye(size, dtype=system.dtype)
    diagonal = jnp.sum(system * eye, axis=1)
    inv_sqrt = lax.rsqrt(diagonal)
    bound = jnp.max(jnp.sum(jnp.abs(system) * inv_sqrt[:, None] * inv_sqrt[None, :], axis=1))
    start = eye * (1.0 / (diagonal * bound))[None, :]

    def going(carry):
        step, _, residual = carry
        return (step < most_steps) & (residual > tolerance)

    def one_step(inverse):
        remainder = eye - jnp.dot(system, inverse, precision=HIGHEST)
        residual = jnp.sqrt(jnp.sum(remainder * remainder))
        return inverse + jnp.dot(inverse, remainder, precision=HIGHEST), residual

    def advance(carry):
        step, inverse, _ = carry
        inverse, _ = one_step(inverse)
        inverse, residual = one_step(inverse)
        return step + 2, inverse, residual

    _, inverse, _ = lax.while_loop(
        going, advance, (jnp.int32(0), start, jnp.array(jnp.inf, system.dtype))
    )
    solved = jnp.dot(inverse, right, precision=HIGHEST)
    return solved + jnp.dot(
        inverse, right - jnp.dot(system, solved, precision=HIGHEST), precision=HIGHEST
    )


def body(
    train_hidden,
    train_outgrad,
    train_mask,
    query_hidden,
    query_outgrad,
    query_mask,
    proj_in,
    proj_out,
):
    train_sketch = sketch_terms(train_hidden, train_outgrad, train_mask, proj_in, proj_out)
    query_sketch = sketch_terms(query_hidden, query_outgrad, query_mask, proj_in, proj_out)
    block_rows = train_sketch.shape[0]
    width = train_sketch.shape[1]
    both = jnp.concatenate([train_sketch, query_sketch], axis=0)
    within = lax.all_gather(both.reshape(1, -1), AXES[1], axis=0, tiled=True)
    everyone = lax.all_gather(within, AXES[0], axis=0, tiled=True)
    devices = everyone.shape[0]
    pieces = [everyone[:, r * width:(r + 1) * width] for r in range(block_rows + 1)]
    gram_matrix = jnp.concatenate(
        [
            jnp.concatenate(
                [jnp.dot(pieces[r], pieces[c].T, precision=HIGHEST) for c in range(block_rows)],
                axis=1,
            )
            for r in range(block_rows)
        ],
        axis=0,
    )
    products = jnp.concatenate(
        [jnp.dot(pieces[r], pieces[block_rows].T, precision=HIGHEST) for r in range(block_rows)],
        axis=0,
    )
    total_rows = gram_matrix.shape[0]
    eye = jnp.eye(total_rows, dtype=jnp.float32)
    damping = damping_share * jnp.sum(gram_matrix * eye) / total_rows
    system = gram_matrix + damping * eye
    system, products = lax.optimization_barrier((system, products))
    solved = total_rows * spd_solve(system, products)
    me = lax.axis_index(AXES)
    return jnp.concatenate(
        [lax.dynamic_slice_in_dim(solved, r * devices + me, 1, 0) for r in range(block_rows)],
        axis=0,
    )


def solution(mesh):
    in_specs = (
        P(AXES, None, None),
        P(AXES, None, None),
        P(AXES, None),
        P(AXES, None, None),
        P(AXES, None, None),
        P(AXES, None),
        P(),
        P(),
    )
    out_specs = P(AXES, None)
    return jax.shard_map(body, mesh=mesh, in_specs=in_specs, out_specs=out_specs, check_vma=False)
```

```python
import jax
import jax.numpy as jnp
from jax import lax
from jax.sharding import PartitionSpec as P

damping_share = 0.1
AXES = ("train", "query")
HIGHEST = lax.Precision.HIGHEST


def sketch_terms(hidden, outgrad, mask, proj_in, proj_out):
    proof_count, token_count, model_width = hidden.shape
    input_side = jnp.dot(
        hidden.reshape(proof_count * token_count, model_width),
        proj_in,
        preferred_element_type=jnp.float32,
    )
    output_side = jnp.dot(
        outgrad.reshape(proof_count * token_count, -1), proj_out, preferred_element_type=jnp.float32
    )
    output_side = output_side * mask.reshape(-1, 1).astype(jnp.float32)
    input_side = input_side.reshape(proof_count, token_count, -1)
    output_side = output_side.reshape(proof_count, token_count, -1)
    outer_sum = jnp.einsum("pti,ptj->pij", output_side, input_side, precision=HIGHEST)
    return outer_sum.reshape(proof_count, -1)


def spd_solve(system, right, tolerance=1e-3, most_steps=48):
    size = system.shape[0]
    eye = jnp.eye(size, dtype=system.dtype)
    diagonal = jnp.sum(system * eye, axis=1)
    inv_sqrt = lax.rsqrt(diagonal)
    bound = jnp.max(jnp.sum(jnp.abs(system) * inv_sqrt[:, None] * inv_sqrt[None, :], axis=1))
    start = eye * (1.0 / (diagonal * bound))[None, :]

    def going(carry):
        step, _, residual = carry
        return (step < most_steps) & (residual > tolerance)

    def one_step(inverse):
        remainder = eye - jnp.dot(system, inverse, precision=HIGHEST)
        residual = jnp.sqrt(jnp.sum(remainder * remainder))
        return inverse + jnp.dot(inverse, remainder, precision=HIGHEST), residual

    def advance(carry):
        step, inverse, _ = carry
        inverse, _ = one_step(inverse)
        inverse, residual = one_step(inverse)
        return step + 2, inverse, residual

    _, inverse, _ = lax.while_loop(
        going, advance, (jnp.int32(0), start, jnp.array(jnp.inf, system.dtype))
    )
    solved = jnp.dot(inverse, right, precision=HIGHEST)
    return solved + jnp.dot(
        inverse, right - jnp.dot(system, solved, precision=HIGHEST), precision=HIGHEST
    )


def body(
    train_hidden,
    train_outgrad,
    train_mask,
    query_hidden,
    query_outgrad,
    query_mask,
    proj_in,
    proj_out,
):
    train_sketch = sketch_terms(train_hidden, train_outgrad, train_mask, proj_in, proj_out)
    query_sketch = sketch_terms(query_hidden, query_outgrad, query_mask, proj_in, proj_out)
    block_rows = train_sketch.shape[0]
    width = train_sketch.shape[1]
    both = jnp.concatenate([train_sketch, query_sketch], axis=0)
    within = lax.all_gather(both.reshape(1, -1), AXES[1], axis=0, tiled=True)
    everyone = lax.all_gather(within, AXES[0], axis=0, tiled=True)
    devices = everyone.shape[0]
    pieces = [everyone[:, r * width:(r + 1) * width] for r in range(block_rows + 1)]
    all_train = jnp.concatenate(pieces[:block_rows], axis=0)
    gram_matrix = jnp.dot(all_train, all_train.T, precision=HIGHEST)
    products = jnp.dot(all_train, pieces[block_rows].T, precision=HIGHEST)
    total_rows = gram_matrix.shape[0]
    eye = jnp.eye(total_rows, dtype=jnp.float32)
    damping = damping_share * jnp.sum(gram_matrix * eye) / total_rows
    system = gram_matrix + damping * eye
    system, products = lax.optimization_barrier((system, products))
    solved = total_rows * spd_solve(system, products)
    me = lax.axis_index(AXES)
    return jnp.concatenate(
        [lax.dynamic_slice_in_dim(solved, r * devices + me, 1, 0) for r in range(block_rows)],
        axis=0,
    )


def solution(mesh):
    in_specs = (
        P(AXES, None, None),
        P(AXES, None, None),
        P(AXES, None),
        P(AXES, None, None),
        P(AXES, None, None),
        P(AXES, None),
        P(),
        P(),
    )
    out_specs = P(AXES, None)
    return jax.shard_map(body, mesh=mesh, in_specs=in_specs, out_specs=out_specs, check_vma=False)
```

```python
import jax
import jax.numpy as jnp
from jax import lax
from jax.sharding import PartitionSpec as P

damping_share = 0.1
AXES = ("train", "query")
HIGHEST = lax.Precision.HIGHEST


def sketch_terms(hidden, outgrad, mask, proj_in, proj_out):
    proof_count, token_count, model_width = hidden.shape
    input_side = jnp.dot(
        hidden.reshape(proof_count * token_count, model_width),
        proj_in,
        preferred_element_type=jnp.float32,
    )
    output_side = jnp.dot(
        outgrad.reshape(proof_count * token_count, -1), proj_out, preferred_element_type=jnp.float32
    )
    output_side = output_side * mask.reshape(-1, 1).astype(jnp.float32)
    input_side = input_side.reshape(proof_count, token_count, -1)
    output_side = output_side.reshape(proof_count, token_count, -1)
    outer_sum = jnp.einsum("pti,ptj->pij", output_side, input_side, precision=HIGHEST)
    return outer_sum.reshape(proof_count, -1)


def spd_solve(system, right, tolerance=1e-3, most_steps=48):
    size = system.shape[0]
    eye = jnp.eye(size, dtype=system.dtype)
    diagonal = jnp.sum(system * eye, axis=1)
    inv_sqrt = lax.rsqrt(diagonal)
    bound = jnp.max(jnp.sum(jnp.abs(system) * inv_sqrt[:, None] * inv_sqrt[None, :], axis=1))
    start = eye * (1.0 / (diagonal * bound))[None, :]

    def going(carry):
        step, _, residual = carry
        return (step < most_steps) & (residual > tolerance)

    def one_step(inverse):
        remainder = eye - jnp.dot(system, inverse, precision=HIGHEST)
        residual = jnp.sqrt(jnp.sum(remainder * remainder))
        return inverse + jnp.dot(inverse, remainder, precision=HIGHEST), residual

    def advance(carry):
        step, inverse, _ = carry
        for _ in range(3):
            inverse, _ = one_step(inverse)
        inverse, residual = one_step(inverse)
        return step + 4, inverse, residual

    _, inverse, _ = lax.while_loop(
        going, advance, (jnp.int32(0), start, jnp.array(jnp.inf, system.dtype))
    )
    solved = jnp.dot(inverse, right, precision=HIGHEST)
    return solved + jnp.dot(
        inverse, right - jnp.dot(system, solved, precision=HIGHEST), precision=HIGHEST
    )


def body(
    train_hidden,
    train_outgrad,
    train_mask,
    query_hidden,
    query_outgrad,
    query_mask,
    proj_in,
    proj_out,
):
    train_sketch = sketch_terms(train_hidden, train_outgrad, train_mask, proj_in, proj_out)
    query_sketch = sketch_terms(query_hidden, query_outgrad, query_mask, proj_in, proj_out)
    block_rows = train_sketch.shape[0]
    width = train_sketch.shape[1]
    both = jnp.concatenate([train_sketch, query_sketch], axis=0)
    within = lax.all_gather(both.reshape(1, -1), AXES[1], axis=0, tiled=True)
    everyone = lax.all_gather(within, AXES[0], axis=0, tiled=True)
    devices = everyone.shape[0]
    pieces = [everyone[:, r * width:(r + 1) * width] for r in range(block_rows + 1)]
    all_train = jnp.concatenate(pieces[:block_rows], axis=0)
    gram_matrix = jnp.dot(all_train, all_train.T, precision=HIGHEST)
    products = jnp.dot(all_train, pieces[block_rows].T, precision=HIGHEST)
    total_rows = gram_matrix.shape[0]
    eye = jnp.eye(total_rows, dtype=jnp.float32)
    damping = damping_share * jnp.sum(gram_matrix * eye) / total_rows
    system = gram_matrix + damping * eye
    system, products = lax.optimization_barrier((system, products))
    solved = total_rows * spd_solve(system, products)
    me = lax.axis_index(AXES)
    return jnp.concatenate(
        [lax.dynamic_slice_in_dim(solved, r * devices + me, 1, 0) for r in range(block_rows)],
        axis=0,
    )


def solution(mesh):
    in_specs = (
        P(AXES, None, None),
        P(AXES, None, None),
        P(AXES, None),
        P(AXES, None, None),
        P(AXES, None, None),
        P(AXES, None),
        P(),
        P(),
    )
    out_specs = P(AXES, None)
    return jax.shard_map(body, mesh=mesh, in_specs=in_specs, out_specs=out_specs, check_vma=False)
```

```python
import jax
import jax.numpy as jnp
from jax import lax
from jax.sharding import PartitionSpec as P

damping_share = 0.1
AXES = ("train", "query")
HIGHEST = lax.Precision.HIGHEST


def sketch_terms(hidden, outgrad, mask, proj_in, proj_out):
    proof_count, token_count, model_width = hidden.shape
    input_side = jnp.dot(
        hidden.reshape(proof_count * token_count, model_width),
        proj_in,
        preferred_element_type=jnp.float32,
    )
    output_side = jnp.dot(
        outgrad.reshape(proof_count * token_count, -1), proj_out, preferred_element_type=jnp.float32
    )
    output_side = output_side * mask.reshape(-1, 1).astype(jnp.float32)
    input_side = input_side.reshape(proof_count, token_count, -1)
    output_side = output_side.reshape(proof_count, token_count, -1)
    outer_sum = jnp.einsum("pti,ptj->pij", output_side, input_side, precision=HIGHEST)
    return outer_sum.reshape(proof_count, -1)


def spd_solve(system, right, tolerance=1e-3, most_steps=48):
    size = system.shape[0]
    eye = jnp.eye(size, dtype=system.dtype)
    diagonal = jnp.sum(system * eye, axis=1)
    inv_sqrt = lax.rsqrt(diagonal)
    bound = jnp.max(jnp.sum(jnp.abs(system) * inv_sqrt[:, None] * inv_sqrt[None, :], axis=1))
    start = eye * (1.0 / (diagonal * bound))[None, :]

    def going(carry):
        step, _, residual = carry
        return (step < most_steps) & (residual > tolerance)

    def one_step(inverse):
        remainder = eye - jnp.dot(system, inverse, precision=HIGHEST)
        residual = jnp.sqrt(jnp.sum(remainder * remainder))
        return inverse + jnp.dot(inverse, remainder, precision=HIGHEST), residual

    def advance(carry):
        step, inverse, _ = carry
        for _ in range(3):
            inverse, _ = one_step(inverse)
        inverse, residual = one_step(inverse)
        return step + 4, inverse, residual

    _, inverse, _ = lax.while_loop(
        going, advance, (jnp.int32(0), start, jnp.array(jnp.inf, system.dtype))
    )
    solved = jnp.dot(inverse, right, precision=HIGHEST)
    return solved + jnp.dot(
        inverse, right - jnp.dot(system, solved, precision=HIGHEST), precision=HIGHEST
    )


def body(
    train_hidden,
    train_outgrad,
    train_mask,
    query_hidden,
    query_outgrad,
    query_mask,
    proj_in,
    proj_out,
):
    train_sketch = sketch_terms(train_hidden, train_outgrad, train_mask, proj_in, proj_out)
    query_sketch = sketch_terms(query_hidden, query_outgrad, query_mask, proj_in, proj_out)
    block_rows = train_sketch.shape[0]
    width = train_sketch.shape[1]
    both = jnp.concatenate([train_sketch, query_sketch], axis=0)
    within = lax.all_gather(both.reshape(1, -1), AXES[0], axis=0, tiled=True)
    everyone = lax.all_gather(within, AXES[1], axis=0, tiled=True)
    devices = everyone.shape[0]
    pieces = [everyone[:, r * width:(r + 1) * width] for r in range(block_rows + 1)]
    all_train = jnp.concatenate(pieces[:block_rows], axis=0)
    gram_matrix = jnp.dot(all_train, all_train.T, precision=HIGHEST)
    products = jnp.dot(all_train, pieces[block_rows].T, precision=HIGHEST)
    total_rows = gram_matrix.shape[0]
    products = products.reshape(total_rows, lax.axis_size(AXES[1]), lax.axis_size(AXES[0]))
    products = products.transpose(0, 2, 1).reshape(total_rows, -1)
    eye = jnp.eye(total_rows, dtype=jnp.float32)
    damping = damping_share * jnp.sum(gram_matrix * eye) / total_rows
    system = gram_matrix + damping * eye
    system, products = lax.optimization_barrier((system, products))
    solved = total_rows * spd_solve(system, products)
    me = lax.axis_index(AXES[1]) * lax.axis_size(AXES[0]) + lax.axis_index(AXES[0])
    return jnp.concatenate(
        [lax.dynamic_slice_in_dim(solved, r * devices + me, 1, 0) for r in range(block_rows)],
        axis=0,
    )


def solution(mesh):
    in_specs = (
        P(AXES, None, None),
        P(AXES, None, None),
        P(AXES, None),
        P(AXES, None, None),
        P(AXES, None, None),
        P(AXES, None),
        P(),
        P(),
    )
    out_specs = P(AXES, None)
    return jax.shard_map(body, mesh=mesh, in_specs=in_specs, out_specs=out_specs, check_vma=False)
```
